32 devices in a mesh: ctx: 8 (over y, x, core), ch: 4 (over z).
Axes of the slice: x: 2, y: 2, z: 4, core: 2. Of those that a mesh axis runs over, the one named last changes fastest.
Arguments:
- query_input: bfloat16 [1024, 4608], P('ctx', 'ch'), may hold values from -6 to 6
- key_input: bfloat16 [1024, 4608], P('ctx', 'ch'), may hold values from -6 to 6
- value_input: bfloat16 [1024, 4608], P('ctx', 'ch'), may hold values from -6 to 6
- filters: bfloat16 [4608, 128], P('ch'), may hold values from -1.7 to 1.7
- complement: int32 [4608], P('ch'), may hold values from 0 to 4607, as said below
- doc_lengths: int32 [16], replicated, may hold values from 1 to 256, 1024 in all
- cotangent: bfloat16 [1024, 4608], P('ctx', 'ch'), may hold values from -6 to 6
Outputs:
- mixer_out: bfloat16 [1024, 4608], P('ctx', 'ch')
- grad_query: bfloat16 [1024, 4608], P('ctx', 'ch')
- grad_key: bfloat16 [1024, 4608], P('ctx', 'ch')
- grad_value: bfloat16 [1024, 4608], P('ctx', 'ch')
- grad_filter: float32 [4608, 128], P('ch', 'ctx')
The draws below stay inside these ranges and needn't reach their ends.
Inputs may be any that keep to these rules, and one draw needn't show every extreme that they name: complement pairs the channels: complement[complement[c]] = c and complement[c] != c for every channel c. `doc_lengths`: the 16 lengths sum to 1024.
All inputs are finite; a program needn't handle non-finite values.
Results may differ from the reference program's by a relative error of at most 0.0065.
Values may be sent and summed in bfloat16 or wider, within the bound.
A program may use at most 192 MiB of HBM per device.

```python
import math
import jax
import jax.numpy as jnp
import numpy as np
from jax import lax

D = 4608
TAPS = 128
DOCS = 16
L = 1024


def draw_filters(key, part):
    key_scale, key_taps = jax.random.split(key)
    low_end = math.log(12.0)
    high_end = math.log(512.0)
    spans = jnp.exp(jax.random.uniform(key_scale, (D, 1), jnp.float32, low_end, high_end))
    offsets = jnp.arange(TAPS, dtype=jnp.float32)[None, :]
    noise = jax.random.truncated_normal(key_taps, -4.0, 4.0, (D, TAPS), jnp.float32)
    values = noise * jnp.exp(-offsets / spans) * jnp.sqrt(2.0 / spans)
    return values.astype(jnp.bfloat16)


def draw_complement(key, part):
    order = jax.random.permutation(key, D).astype(jnp.int32)
    leaders = order[0::2]
    partners = order[1::2]
    table = jnp.zeros((D,), jnp.int32).at[leaders].set(partners).at[partners].set(leaders)
    return table.astype(jnp.int32)


def block_levels(key, extent, cuts, low, top_value):
    gain, own = 1.0, jax.random.fold_in(key, 6)
    for dim, blocks in cuts:
        heights = jnp.exp(jax.random.uniform(jax.random.fold_in(own, dim), (blocks,), jnp.float32, low / len(cuts), top_value / len(cuts)))
        gain = gain * jnp.repeat(heights, extent[dim] // blocks).reshape([-1 if axis == dim else 1 for axis in range(len(extent))])
    return gain


def split_up(count, total, most, skew):
    loads = [(1 << 20) // math.isqrt(rank ** skew) + 1 for rank in range(2, count + 1)]
    rest, holding = total - most - (count - 1), [1] * (count - 1)
    while rest > 0:
        candidates = [i for i in range(count - 1) if holding[i] < most]
        pool, budget = sum([loads[i] for i in candidates]), rest
        for i in candidates:
            addition = min(most - holding[i], max(1, budget * loads[i] // pool), rest)
            holding[i] = holding[i] + addition
            rest = rest - addition
    return np.array([most] + holding)


def ragged_sizes(rng, amount, total, most, lean):
    if amount == 2:
        one = jax.random.randint(rng, (), max(1, total - most), min(most, total - 1) + 1)
        return jnp.stack([one, total - one])
    sizes = jnp.asarray(split_up(amount, total, most, lean), jnp.int32)
    pairs = (amount - 1) // 2
    giver, taker = sizes[1:1 + 2 * pairs:2], sizes[2:2 + 2 * pairs:2]
    room = jnp.minimum(giver - 1, most - taker)
    shifted = jax.random.randint(jax.random.fold_in(rng, 1), (pairs,), 0, 1 << 20) % (room + 1)
    sizes = sizes.at[1:1 + 2 * pairs:2].set(giver - shifted).at[2:2 + 2 * pairs:2].set(taker + shifted)
    return sizes[jax.random.permutation(jax.random.fold_in(rng, 2), amount)]


def normal_values(key, dims, scale, bound, cuts=(), kind=jnp.bfloat16):
    array = jax.random.normal(key, dims, jnp.float32) * scale
    if len(cuts) > 0:
        array = block_levels(key, dims, cuts, -0.22, 0.18) * array
    return jnp.clip(array, min=-bound, max=bound).astype(kind)


def setup_inputs(seed: int = 0) -> dict:
    key_list = jax.random.split(jax.random.key(seed), 8)
    query_input = normal_values(key_list[0], (L, D), 1.0, 6.0, ((0, 8), (1, 4)))
    key_input = normal_values(key_list[1], (L, D), 1.0, 6.0, ((0, 8), (1, 4)))
    value_input = normal_values(key_list[2], (L, D), 1.0, 6.0, ((0, 8), (1, 4)))
    filters = draw_filters(jax.random.fold_in(key_list[7], 71), 0)
    complement = draw_complement(jax.random.fold_in(key_list[7], 71), 0)
    doc_lengths = ragged_sizes(key_list[5], DOCS, L, L // 4, 0).astype(jnp.int32)
    cotangent = normal_values(key_list[6], (L, D), 1.0, 6.0, ((0, 8), (1, 4)))
    return dict(query_input=query_input, key_input=key_input, value_input=value_input, filters=filters, complement=complement, doc_lengths=doc_lengths, cotangent=cotangent)


def reference(query_input, key_input, value_input, filters, complement, doc_lengths, cotangent):
    rim_width = TAPS - 1
    places = jnp.arange(L, dtype=jnp.int32)
    doc_ends = jnp.cumsum(doc_lengths).astype(jnp.int32)
    starts = doc_ends - doc_lengths
    inside = (places[:, None] >= starts[None, :]) & (places[:, None] < doc_ends[None, :])
    doc_first = jnp.sum(jnp.where(inside, starts[None, :], 0), axis=1).astype(jnp.int32)
    doc_last = jnp.sum(jnp.where(inside, doc_ends[None, :] - 1, 0), axis=1).astype(jnp.int32)
    key_f = key_input.astype(jnp.float32)
    value_f = value_input.astype(jnp.float32)
    query_f = query_input.astype(jnp.float32)
    cot_f = cotangent.astype(jnp.float32)
    product = (key_f * value_f).astype(jnp.bfloat16)
    kernel_t = filters.astype(jnp.float32).T
    partner_t = filters.astype(jnp.float32)[complement].T
    padded_u = jnp.pad(product.astype(jnp.float32), ((rim_width, rim_width), (0, 0)))
    offsets = jnp.arange(TAPS, dtype=jnp.int32)

    def masks(offset):
        behind = (places - offset >= doc_first).astype(jnp.float32)[:, None]
        forward = (places + offset <= doc_last).astype(jnp.float32)[:, None]
        return behind, forward

    def forward_tap(carry, offset):
        causal, anti = carry
        behind, forward = masks(offset)
        earlier = lax.dynamic_slice_in_dim(padded_u, (rim_width - offset).astype(jnp.int32), L, 0)
        later = lax.dynamic_slice_in_dim(padded_u, (rim_width + offset).astype(jnp.int32), L, 0)
        causal = causal + kernel_t[offset][None, :] * earlier * behind
        anti = anti + partner_t[offset][None, :] * later * forward
        return (causal, anti), None

    zeros = jnp.zeros((L, D), jnp.float32)
    (causal, anti), _ = lax.scan(forward_tap, (zeros, zeros), offsets)
    strand_rc = anti.astype(jnp.bfloat16)
    combined = causal + strand_rc.astype(jnp.float32)
    mixer_out = (query_f * combined).astype(jnp.bfloat16)
    grad_query = (cot_f * combined).astype(jnp.bfloat16)
    upstream = (cot_f * query_f).astype(jnp.bfloat16)
    upstream_f = upstream.astype(jnp.float32)
    padded_r = jnp.pad(upstream_f, ((rim_width, rim_width), (0, 0)))

    def backward_tap(carry, offset):
        ahead_sum, behind_sum = carry
        behind, forward = masks(offset)
        low = (rim_width - offset).astype(jnp.int32)
        high = (rim_width + offset).astype(jnp.int32)
        earlier_u = lax.dynamic_slice_in_dim(padded_u, low, L, 0)
        later_u = lax.dynamic_slice_in_dim(padded_u, high, L, 0)
        earlier_r = lax.dynamic_slice_in_dim(padded_r, low, L, 0)
        later_r = lax.dynamic_slice_in_dim(padded_r, high, L, 0)
        ahead_sum = ahead_sum + kernel_t[offset][None, :] * later_r * forward
        behind_sum = behind_sum + partner_t[offset][None, :] * earlier_r * behind
        own = jnp.sum(upstream_f * earlier_u * behind, axis=0)
        mirrored = jnp.sum(upstream_f * later_u * forward, axis=0)
        return (ahead_sum, behind_sum), (own, mirrored)

    (ahead_sum, behind_sum), (own_rows, mirrored_rows) = lax.scan(backward_tap, (zeros, zeros), offsets)
    rc_grad = behind_sum.astype(jnp.bfloat16)
    grad_product = ahead_sum + rc_grad.astype(jnp.float32)
    grad_key = (grad_product * value_f).astype(jnp.bfloat16)
    grad_value = (grad_product * key_f).astype(jnp.bfloat16)
    grad_filter = (own_rows + mirrored_rows[:, complement]).T.astype(jnp.float32)
    return (mixer_out, grad_query, grad_key, grad_value, grad_filter)
```

```python
import functools

import jax
import jax.numpy as jnp
import numpy as np
from jax import lax
from jax.experimental import pallas as pl
from jax.experimental.pallas import tpu as pltpu
from jax.sharding import PartitionSpec as P

F32, BF16 = jnp.float32, jnp.bfloat16


def split_bf16(table):
    high = table.astype(BF16)
    low = (table - high.astype(np.float64)).astype(BF16)
    return high, low


def fourier_tables(rows, taps, owners):
    length = 3 * rows
    angle = 2.0 * np.pi * (np.arange(length // 2) + 0.5) / length
    places = np.arange(length) - rows
    turns = angle[:, None] * places[None, :]
    analyse = np.concatenate([np.cos(turns), -np.sin(turns)], axis=0)
    own = np.arange(rows)[:, None] * angle[None, :]
    rebuild = np.concatenate([np.cos(own), -np.sin(own)], axis=1) * (2.0 / length)
    lags = angle[:, None] * np.arange(taps)[None, :]
    causal = np.concatenate([np.cos(lags), -np.sin(lags)], axis=0)
    anti = np.concatenate([np.cos(lags), np.sin(lags)], axis=0)
    share = taps // owners
    offsets = np.concatenate([
        np.concatenate([np.arange(t * share, (t + 1) * share), -np.arange(t * share, (t + 1) * share)])
        for t in range(owners)
    ])
    spread = offsets[:, None] * angle[None, :]
    tap_rows = np.concatenate([np.cos(spread), -np.sin(spread)], axis=1) * (2.0 / length)
    return (
        analyse.astype(BF16),
        rebuild.astype(BF16),
        *split_bf16(causal),
        *split_bf16(anti),
        *split_bf16(tap_rows),
    )


def mm(a, b):
    return jnp.dot(a, b, preferred_element_type=F32)


def mm_t(a, b):
    return lax.dot_general(a, b, (((1,), (1,)), ((), ())), preferred_element_type=F32)


def mix_kernel(
    lens, query, key, value, cot, u_prev, u_next, r_prev, r_next, taps_own, taps_partner,
    analyse, rebuild, causal_hi, causal_lo, anti_hi, anti_lo, tap_hi, tap_lo,
    mixer_out, grad_query, grad_key, grad_value, tap_sums,
    spectrum, window_u, own_r, acc_y, acc_p, acc_g, z_ref, q_ref,
):
    rows = query.shape[0]
    half = analyse.shape[0] // 2
    first_place = lax.axis_index("ctx") * rows

    f, g = taps_own[...], taps_partner[...]
    spectrum[...] = (
        mm_t(causal_hi[...], f) + mm_t(causal_lo[...], f) + mm_t(anti_hi[...], g) + mm_t(anti_lo[...], g)
    )
    window_u[0:rows] = u_prev[...]
    window_u[rows : 2 * rows] = (key[...].astype(F32) * value[...].astype(F32)).astype(BF16)
    window_u[2 * rows : 3 * rows] = u_next[...]
    own_r[...] = (cot[...].astype(F32) * query[...].astype(F32)).astype(BF16)
    acc_y[...] = jnp.zeros_like(acc_y)
    acc_p[...] = jnp.zeros_like(acc_p)
    acc_g[...] = jnp.zeros_like(acc_g)

    def document(d, start):
        end = start + lens[d]

        @pl.when((start < first_place + rows) & (end > first_place))
        def _():
            low, high = start - first_place, end - first_place
            lane = lax.broadcasted_iota(jnp.int32, (1, 3 * rows), 1) - rows
            here = ((lane >= low) & (lane < high)).astype(F32).astype(BF16)
            masked = analyse[...] * here
            column = lax.broadcasted_iota(jnp.int32, (rows, 1), 0)
            kept = ((column >= low) & (column < high)).astype(F32).astype(BF16)
            back = rebuild[...] * kept
            u_hat = mm(masked, window_u[...])
            o_hat = mm(masked[:, rows : 2 * rows], own_r[...])
            r_hat = o_hat + mm(masked[:, :rows], r_prev[...]) + mm(masked[:, 2 * rows :], r_next[...])
            h_re, h_im = spectrum[:half], spectrum[half:]
            u_re, u_im = u_hat[:half], u_hat[half:]
            r_re, r_im = r_hat[:half], r_hat[half:]
            o_re, o_im = o_hat[:half], o_hat[half:]
            z_ref[:half] = (h_re * u_re - h_im * u_im).astype(BF16)
            z_ref[half:] = (h_re * u_im + h_im * u_re).astype(BF16)
            q_ref[:half] = (h_re * r_re + h_im * r_im).astype(BF16)
            q_ref[half:] = (h_re * r_im - h_im * r_re).astype(BF16)
            acc_g[:half] += o_re * u_re + o_im * u_im
            acc_g[half:] += o_im * u_re - o_re * u_im
            acc_y[...] += mm(back, z_ref[...])
            acc_p[...] += mm(back, q_ref[...])

        return end

    lax.fori_loop(0, lens.shape[0], document, jnp.int32(0))
    combined, grad_product = acc_y[...], acc_p[...]
    mixer_out[...] = (query[...].astype(F32) * combined).astype(BF16)
    grad_query[...] = (cot[...].astype(F32) * combined).astype(BF16)
    grad_key[...] = (grad_product * value[...].astype(F32)).astype(BF16)
    grad_value[...] = (grad_product * key[...].astype(F32)).astype(BF16)
    g_sum = acc_g[...]
    g_hi = g_sum.astype(BF16)
    g_lo = (g_sum - g_hi.astype(F32)).astype(BF16)
    tap_sums[...] = mm(tap_hi[...], g_hi) + mm(tap_hi[...], g_lo) + mm(tap_lo[...], g_hi)


def channel_block(channels):
    for block in (384, 256, 128):
        if channels % block == 0:
            return block
    return channels


def mix(doc_lengths, fields, filters, partner, owners):
    rows, channels = fields[0].shape
    taps = filters.shape[1]
    block = channel_block(channels)
    tables = fourier_tables(rows, taps, owners)
    length = 3 * rows
    field_spec = pl.BlockSpec((rows, block), lambda i: (0, i))
    filter_spec = pl.BlockSpec((block, taps), lambda i: (i, 0))
    table_specs = [pl.BlockSpec(t.shape, lambda i: (0, 0)) for t in tables]
    return pl.pallas_call(
        mix_kernel,
        grid=(channels // block,),
        in_specs=[pl.BlockSpec(memory_space=pltpu.SMEM)]
        + [field_spec] * 8
        + [filter_spec] * 2
        + table_specs,
        out_specs=[field_spec] * 4 + [pl.BlockSpec((2 * taps, block), lambda i: (0, i))],
        out_shape=[jax.ShapeDtypeStruct((rows, channels), BF16)] * 4
        + [jax.ShapeDtypeStruct((2 * taps, channels), F32)],
        scratch_shapes=[
            pltpu.VMEM((length, block), F32),
            pltpu.VMEM((length, block), BF16),
            pltpu.VMEM((rows, block), BF16),
            pltpu.VMEM((rows, block), F32),
            pltpu.VMEM((rows, block), F32),
            pltpu.VMEM((length, block), F32),
            pltpu.VMEM((length, block), BF16),
            pltpu.VMEM((length, block), BF16),
        ],
        name="mix",
    )(doc_lengths, *fields, filters, partner, *[jnp.asarray(t) for t in tables])


def gather_relative(shard, axis):
    size = lax.axis_size(axis)
    blocks = [shard]
    for step in range(1, size):
        blocks.append(lax.ppermute(shard, axis, [(i, (i + step) % size) for i in range(size)]))
    return jnp.concatenate(blocks, axis=0)


def reduce_owned(pieces, axis):
    size = lax.axis_size(axis)
    me = lax.axis_index(axis)
    if size > 8:
        return lax.psum_scatter(pieces, axis, scatter_dimension=0, tiled=False)
    total = lax.dynamic_index_in_dim(pieces, me, 0, keepdims=False)
    for step in range(1, size):
        piece = lax.dynamic_index_in_dim(pieces, (me + step) % size, 0, keepdims=False)
        total = total + lax.ppermute(piece, axis, [(i, (i + step) % size) for i in range(size)])
    return total


def shards(query_input, key_input, value_input, filters, complement, doc_lengths, cotangent):
    channels, taps = filters.shape
    ctx, ch = lax.axis_size("ctx"), lax.axis_size("ch")
    up = [(i, i + 1) for i in range(ctx - 1)]
    down = [(j, i) for i, j in up]
    product = (key_input.astype(F32) * value_input.astype(F32)).astype(BF16)
    upstream = (cotangent.astype(F32) * query_input.astype(F32)).astype(BF16)
    halos = [lax.ppermute(field, "ctx", way) for field in (product, upstream) for way in (up, down)]

    place = (lax.axis_index("ch") - complement // channels) % ch * channels + complement % channels
    partner = jnp.take(gather_relative(filters, "ch"), place, axis=0, mode="clip")
    *mixed, tap_sums = mix(
        doc_lengths, (query_input, key_input, value_input, cotangent, *halos), filters, partner, ctx
    )
    share = taps // ctx
    owned = reduce_owned(tap_sums.reshape(ctx, 2 * share, channels), "ctx")
    mirrored = gather_relative(owned[share:].T, "ch")
    grad_filter = owned[:share].T + jnp.take(mirrored, place, axis=0, mode="clip")
    return (*mixed, grad_filter)


def solution(mesh):
    placed = (
        P("ctx", "ch"),
        P("ctx", "ch"),
        P("ctx", "ch"),
        P("ch", None),
        P("ch"),
        P(),
        P("ctx", "ch"),
    )
    return jax.shard_map(
        shards,
        mesh=mesh,
        in_specs=placed,
        out_specs=(P("ctx", "ch"), P("ctx", "ch"), P("ctx", "ch"), P("ctx", "ch"), P("ch", "ctx")),
        check_vma=False,
    )
```

```python
import functools

import jax
import jax.numpy as jnp
import numpy as np
from jax import lax
from jax.experimental import pallas as pl
from jax.experimental.pallas import tpu as pltpu
from jax.sharding import PartitionSpec as P

F32, BF16 = jnp.float32, jnp.bfloat16


def split_bf16(table):
    high = table.astype(BF16)
    low = (table - high.astype(np.float64)).astype(BF16)
    return high, low


def fourier_tables(rows, taps, owners):
    length = 3 * rows
    angle = 2.0 * np.pi * (np.arange(length // 2) + 0.5) / length
    places = np.arange(length) - rows
    turns = angle[:, None] * places[None, :]
    analyse = np.concatenate([np.cos(turns), -np.sin(turns)], axis=0)
    own = np.arange(rows)[:, None] * angle[None, :]
    rebuild = np.concatenate([np.cos(own), -np.sin(own)], axis=1) * (2.0 / length)
    lags = angle[:, None] * np.arange(taps)[None, :]
    causal = np.concatenate([np.cos(lags), -np.sin(lags)], axis=0)
    anti = np.concatenate([np.cos(lags), np.sin(lags)], axis=0)
    share = taps // owners
    offsets = np.concatenate([
        np.concatenate([np.arange(t * share, (t + 1) * share), -np.arange(t * share, (t + 1) * share)])
        for t in range(owners)
    ])
    spread = offsets[:, None] * angle[None, :]
    tap_rows = np.concatenate([np.cos(spread), -np.sin(spread)], axis=1) * (2.0 / length)
    return (
        analyse.astype(BF16),
        rebuild.astype(BF16),
        *split_bf16(causal),
        *split_bf16(anti),
        *split_bf16(tap_rows),
    )


def mm(a, b):
    return jnp.dot(a, b, preferred_element_type=F32)


def mm_t(a, b):
    return lax.dot_general(a, b, (((1,), (1,)), ((), ())), preferred_element_type=F32)


def mix_kernel(
    lens, query, key, value, cot, u_prev, u_next, r_prev, r_next, taps_own, taps_partner,
    analyse, rebuild, causal_hi, causal_lo, anti_hi, anti_lo, tap_hi, tap_lo,
    mixer_out, grad_query, grad_key, grad_value, tap_sums,
    spectrum, window_u, own_r, acc_y, acc_p, acc_g, z_ref, q_ref,
):
    rows = query.shape[0]
    half = analyse.shape[0] // 2
    first_place = lax.axis_index("ctx") * rows

    f, g = taps_own[...], taps_partner[...]
    spectrum[...] = (
        mm_t(causal_hi[...], f) + mm_t(causal_lo[...], f) + mm_t(anti_hi[...], g) + mm_t(anti_lo[...], g)
    )
    window_u[0:rows] = u_prev[...]
    window_u[rows : 2 * rows] = (key[...].astype(F32) * value[...].astype(F32)).astype(BF16)
    window_u[2 * rows : 3 * rows] = u_next[...]
    own_r[...] = (cot[...].astype(F32) * query[...].astype(F32)).astype(BF16)
    acc_y[...] = jnp.zeros_like(acc_y)
    acc_p[...] = jnp.zeros_like(acc_p)
    acc_g[...] = jnp.zeros_like(acc_g)

    def document(d, start):
        end = start + lens[d]

        @pl.when((start < first_place + rows) & (end > first_place))
        def _():
            low, high = start - first_place, end - first_place
            lane = lax.broadcasted_iota(jnp.int32, (1, 3 * rows), 1) - rows
            here = ((lane >= low) & (lane < high)).astype(F32).astype(BF16)
            masked = analyse[...] * here
            column = lax.broadcasted_iota(jnp.int32, (rows, 1), 0)
            kept = ((column >= low) & (column < high)).astype(F32).astype(BF16)
            back = rebuild[...] * kept
            u_hat = mm(masked, window_u[...])
            o_hat = mm(masked[:, rows : 2 * rows], own_r[...])
            r_hat = o_hat + mm(masked[:, :rows], r_prev[...]) + mm(masked[:, 2 * rows :], r_next[...])
            h_re, h_im = spectrum[:half], spectrum[half:]
            u_re, u_im = u_hat[:half], u_hat[half:]
            r_re, r_im = r_hat[:half], r_hat[half:]
            o_re, o_im = o_hat[:half], o_hat[half:]
            z_ref[:half] = (h_re * u_re - h_im * u_im).astype(BF16)
            z_ref[half:] = (h_re * u_im + h_im * u_re).astype(BF16)
            q_ref[:half] = (h_re * r_re + h_im * r_im).astype(BF16)
            q_ref[half:] = (h_re * r_im - h_im * r_re).astype(BF16)
            acc_g[:half] += o_re * u_re + o_im * u_im
            acc_g[half:] += o_im * u_re - o_re * u_im
            acc_y[...] += mm(back, z_ref[...])
            acc_p[...] += mm(back, q_ref[...])

        return end

    lax.fori_loop(0, lens.shape[0], document, jnp.int32(0))
    combined, grad_product = acc_y[...], acc_p[...]
    mixer_out[...] = (query[...].astype(F32) * combined).astype(BF16)
    grad_query[...] = (cot[...].astype(F32) * combined).astype(BF16)
    grad_key[...] = (grad_product * value[...].astype(F32)).astype(BF16)
    grad_value[...] = (grad_product * key[...].astype(F32)).astype(BF16)
    g_sum = acc_g[...]
    g_hi = g_sum.astype(BF16)
    g_lo = (g_sum - g_hi.astype(F32)).astype(BF16)
    sums = mm(tap_hi[...], g_hi) + mm(tap_hi[...], g_lo) + mm(tap_lo[...], g_hi)
    tap_sums[...] = sums.astype(BF16)


def channel_block(channels):
    for block in (384, 256, 128):
        if channels % block == 0:
            return block
    return channels


def mix(doc_lengths, fields, filters, partner, owners):
    rows, channels = fields[0].shape
    taps = filters.shape[1]
    block = channel_block(channels)
    tables = fourier_tables(rows, taps, owners)
    length = 3 * rows
    field_spec = pl.BlockSpec((rows, block), lambda i: (0, i))
    filter_spec = pl.BlockSpec((block, taps), lambda i: (i, 0))
    table_specs = [pl.BlockSpec(t.shape, lambda i: (0, 0)) for t in tables]
    return pl.pallas_call(
        mix_kernel,
        grid=(channels // block,),
        in_specs=[pl.BlockSpec(memory_space=pltpu.SMEM)]
        + [field_spec] * 8
        + [filter_spec] * 2
        + table_specs,
        out_specs=[field_spec] * 4 + [pl.BlockSpec((2 * taps, block), lambda i: (0, i))],
        out_shape=[jax.ShapeDtypeStruct((rows, channels), BF16)] * 4
        + [jax.ShapeDtypeStruct((2 * taps, channels), BF16)],
        scratch_shapes=[
            pltpu.VMEM((length, block), F32),
            pltpu.VMEM((length, block), BF16),
            pltpu.VMEM((rows, block), BF16),
            pltpu.VMEM((rows, block), F32),
            pltpu.VMEM((rows, block), F32),
            pltpu.VMEM((length, block), F32),
            pltpu.VMEM((length, block), BF16),
            pltpu.VMEM((length, block), BF16),
        ],
        name="mix",
    )(doc_lengths, *fields, filters, partner, *[jnp.asarray(t) for t in tables])


def remote(src, dst, sems, index, device):
    return pltpu.make_async_remote_copy(
        src_ref=src, dst_ref=dst, send_sem=sems[0].at[index], recv_sem=sems[1].at[index],
        device_id=device, device_id_type=pl.DeviceIdType.MESH,
    )


def greet(devices):
    barrier = pltpu.get_barrier_semaphore()
    for device in devices:
        pl.semaphore_signal(barrier, inc=1, device_id=device, device_id_type=pl.DeviceIdType.MESH)
    pl.semaphore_wait(barrier, len(devices))


def spread_kernel(ctx, ch, u, r, filters, u_prev, u_next, r_prev, r_next, gathered,
                  halo_send, halo_recv, ch_send, ch_recv, core_send, core_recv, local):
    me, mine = lax.axis_index("ctx"), lax.axis_index("ch")
    after, before = {"ctx": (me + 1) % ctx}, {"ctx": (me + ctx - 1) % ctx}
    parity = me % 2
    twin = {"ctx": me + 1 - 2 * parity}
    rows = filters.shape[0] // 2
    half = pl.ds(pl.multiple_of(parity * rows, rows), rows)
    peers = [{"ch": (mine + step) % ch} for step in range(1, ch)]
    keep = pltpu.make_async_copy(filters, gathered.at[0], local)
    keep.start()
    greet([after, before] + peers)
    wide = [
        remote(filters.at[half], gathered.at[step, half], (ch_send, ch_recv), step - 1, peers[step - 1])
        for step in range(1, ch)
    ]
    for copy in wide[::-1]:
        copy.start()
    halos = [
        remote(field, place, (halo_send, halo_recv), index, device)
        for index, (field, place, device) in enumerate(
            ((u, u_prev, after), (u, u_next, before), (r, r_prev, after), (r, r_next, before))
        )
    ]
    for copy in halos:
        copy.start()
    swaps = []
    for step in range(1, ch):
        wide[step - 1].wait_recv()
        swap = remote(gathered.at[step, half], gathered.at[step, half], (core_send, core_recv), step - 1, twin)
        swap.start()
        swaps.append(swap)
    for copy in swaps:
        copy.wait()
    for copy in wide:
        copy.wait_send()
    for copy in halos:
        copy.wait()
    keep.wait()


def spread(product, upstream, filters):
    ctx, ch = lax.axis_size("ctx"), lax.axis_size("ch")
    hbm = pl.BlockSpec(memory_space=pl.ANY)
    dma = pltpu.SemaphoreType.DMA
    field = jax.ShapeDtypeStruct(product.shape, BF16)
    return pl.pallas_call(
        functools.partial(spread_kernel, ctx, ch),
        in_specs=[hbm] * 3,
        out_specs=[hbm] * 5,
        out_shape=[field] * 4 + [jax.ShapeDtypeStruct((ch, *filters.shape), BF16)],
        scratch_shapes=[dma((4,)), dma((4,)), dma((ch - 1,)), dma((ch - 1,)), dma((ch - 1,)), dma((ch - 1,)), dma],
        compiler_params=pltpu.CompilerParams(collective_id=0, has_side_effects=True),
        name="spread",
    )(product, upstream, filters)


def collect_kernel(ctx, ch, pieces, own, mirrored, landed, sent, got, sum_send, sum_recv, ch_send, ch_recv, local):
    me, mine = lax.axis_index("ctx"), lax.axis_index("ch")
    share = own.shape[0]
    others = [{"ctx": (me + step) % ctx} for step in range(1, ctx)]
    peers = [{"ch": (mine + step) % ch} for step in range(1, ch)]
    keep = pltpu.make_async_copy(pieces.at[me], landed.at[0], local)
    keep.start()
    greet(others + peers)
    copies = [
        remote(pieces.at[(me + step) % ctx], landed.at[step], (sum_send, sum_recv), step - 1, others[step - 1])
        for step in range(1, ctx)
    ]
    for copy in copies:
        copy.start()
    keep.wait()
    for copy in copies:
        copy.wait()
    sent[...] = sum(landed[step, share:].astype(F32) for step in range(ctx)).astype(BF16)
    own[...] = sum(landed[step, :share].astype(F32) for step in range(ctx))
    copies = [
        remote(sent, got.at[step - 1], (ch_send, ch_recv), step - 1, peers[step - 1]) for step in range(1, ch)
    ]
    for copy in copies:
        copy.start()
    mirrored[0] = sent[...]
    for step, copy in enumerate(copies):
        copy.wait()
        mirrored[step + 1] = got[step]


def collect(pieces):
    ctx, ch = lax.axis_size("ctx"), lax.axis_size("ch")
    _, double, channels = pieces.shape
    share = double // 2
    vmem = pl.BlockSpec(memory_space=pltpu.VMEM)
    dma = pltpu.SemaphoreType.DMA
    return pl.pallas_call(
        functools.partial(collect_kernel, ctx, ch),
        in_specs=[pl.BlockSpec(memory_space=pl.ANY)],
        out_specs=[vmem] * 2,
        out_shape=[
            jax.ShapeDtypeStruct((share, channels), F32),
            jax.ShapeDtypeStruct((ch, share, channels), BF16),
        ],
        scratch_shapes=[
            pltpu.VMEM((ctx, double, channels), BF16),
            pltpu.VMEM((share, channels), BF16),
            pltpu.VMEM((ch - 1, share, channels), BF16),
            dma((ctx - 1,)), dma((ctx - 1,)), dma((ch - 1,)), dma((ch - 1,)), dma,
        ],
        compiler_params=pltpu.CompilerParams(collective_id=1, has_side_effects=True),
        name="collect",
    )(pieces)


def shards(query_input, key_input, value_input, filters, complement, doc_lengths, cotangent):
    channels, taps = filters.shape
    ctx, ch = lax.axis_size("ctx"), lax.axis_size("ch")
    product = (key_input.astype(F32) * value_input.astype(F32)).astype(BF16)
    upstream = (cotangent.astype(F32) * query_input.astype(F32)).astype(BF16)
    *halos, gathered = spread(product, upstream, filters)

    place = (lax.axis_index("ch") - complement // channels) % ch * channels + complement % channels
    partner = jnp.take(gathered.reshape(ch * channels, taps), place, axis=0, mode="clip")
    *mixed, tap_sums = mix(
        doc_lengths, (query_input, key_input, value_input, cotangent, *halos), filters, partner, ctx
    )
    share = taps // ctx
    own, mirrored = collect(tap_sums.reshape(ctx, 2 * share, channels))
    mirrored = jnp.swapaxes(mirrored, 1, 2).reshape(ch * channels, share)
    grad_filter = own.T + jnp.take(mirrored, place, axis=0, mode="clip").astype(F32)
    return (*mixed, grad_filter)


def solution(mesh):
    placed = (
        P("ctx", "ch"),
        P("ctx", "ch"),
        P("ctx", "ch"),
        P("ch", None),
        P("ch"),
        P(),
        P("ctx", "ch"),
    )
    return jax.shard_map(
        shards,
        mesh=mesh,
        in_specs=placed,
        out_specs=(P("ctx", "ch"), P("ctx", "ch"), P("ctx", "ch"), P("ctx", "ch"), P("ch", "ctx")),
        check_vma=False,
    )
```

```python
import functools

import jax
import jax.numpy as jnp
import numpy as np
from jax import lax
from jax.experimental import pallas as pl
from jax.experimental.pallas import tpu as pltpu
from jax.sharding import PartitionSpec as P

F32, BF16 = jnp.float32, jnp.bfloat16


def split_bf16(table):
    high = table.astype(BF16)
    low = (table - high.astype(np.float64)).astype(BF16)
    return high, low


def fourier_tables(rows, taps, owners):
    length = 3 * rows
    angle = 2.0 * np.pi * (np.arange(length // 2) + 0.5) / length
    places = np.concatenate([np.arange(rows), np.arange(rows) - rows, np.arange(rows) + rows])
    turns = angle[:, None] * places[None, :]
    analyse = np.concatenate([np.cos(turns), -np.sin(turns)], axis=0)
    own = np.arange(rows)[:, None] * angle[None, :]
    rebuild = np.concatenate([np.cos(own), -np.sin(own)], axis=1) * (2.0 / length)
    lags = angle[:, None] * np.arange(taps)[None, :]
    causal = np.concatenate([np.cos(lags), -np.sin(lags)], axis=0)
    anti = np.concatenate([np.cos(lags), np.sin(lags)], axis=0)
    share = taps // owners
    offsets = np.concatenate([
        np.concatenate([np.arange(t * share, (t + 1) * share), -np.arange(t * share, (t + 1) * share)])
        for t in range(owners)
    ])
    spread = offsets[:, None] * angle[None, :]
    tap_rows = np.concatenate([np.cos(spread), -np.sin(spread)], axis=1) * (2.0 / length)
    return (
        analyse.astype(BF16),
        rebuild.astype(BF16),
        *split_bf16(causal),
        *split_bf16(anti),
        *split_bf16(tap_rows),
    )


def mm(a, b):
    return jnp.dot(a, b, preferred_element_type=F32)


def mm_t(a, b):
    return lax.dot_general(a, b, (((1,), (1,)), ((), ())), preferred_element_type=F32)


def mix_kernel(
    lens, query, key, value, cot, u_prev, u_next, r_prev, r_next, taps_own, taps_partner,
    analyse, rebuild, causal_hi, causal_lo, anti_hi, anti_lo, tap_hi, tap_lo,
    mixer_out, grad_query, grad_key, grad_value, tap_sums,
    spectrum, own_pair, halo_pair, acc, acc_g, pair_hat,
):
    rows = query.shape[0]
    half = analyse.shape[0] // 2
    first_place = lax.axis_index("ctx") * rows

    f, g = taps_own[...], taps_partner[...]
    spectrum[...] = (
        mm_t(causal_hi[...], f) + mm_t(causal_lo[...], f) + mm_t(anti_hi[...], g) + mm_t(anti_lo[...], g)
    )
    block = query.shape[1]
    left, right = pl.ds(0, block), pl.ds(block, block)
    own_pair[:, left] = (key[...].astype(F32) * value[...].astype(F32)).astype(BF16)
    own_pair[:, right] = (cot[...].astype(F32) * query[...].astype(F32)).astype(BF16)
    halo_pair[:rows, left] = u_prev[...]
    halo_pair[rows:, left] = u_next[...]
    halo_pair[:rows, right] = r_prev[...]
    halo_pair[rows:, right] = r_next[...]
    acc[...] = jnp.zeros_like(acc)
    acc_g[...] = jnp.zeros_like(acc_g)

    def document(d, start):
        end = start + lens[d]

        @pl.when((start < first_place + rows) & (end > first_place))
        def _():
            low, high = start - first_place, end - first_place
            lane = lax.broadcasted_iota(jnp.int32, (1, 3 * rows), 1)
            lane = jnp.where(lane < rows, lane, jnp.where(lane < 2 * rows, lane - 2 * rows, lane - rows))
            here = ((lane >= low) & (lane < high)).astype(F32).astype(BF16)
            masked = analyse[...] * here
            column = lax.broadcasted_iota(jnp.int32, (rows, 1), 0)
            kept = ((column >= low) & (column < high)).astype(F32).astype(BF16)
            back = rebuild[...] * kept
            own_hat = mm(masked[:, :rows], own_pair[...])
            hat = own_hat + mm(masked[:, rows:], halo_pair[...])
            h_re, h_im = spectrum[:half], spectrum[half:]
            u_re, u_im = hat[:half, :block], hat[half:, :block]
            r_re, r_im = hat[:half, block:], hat[half:, block:]
            o_re, o_im = own_hat[:half, block:], own_hat[half:, block:]
            pair_hat[:half, left] = (h_re * u_re - h_im * u_im).astype(BF16)
            pair_hat[half:, left] = (h_re * u_im + h_im * u_re).astype(BF16)
            pair_hat[:half, right] = (h_re * r_re + h_im * r_im).astype(BF16)
            pair_hat[half:, right] = (h_re * r_im - h_im * r_re).astype(BF16)
            acc_g[:half] += o_re * u_re + o_im * u_im
            acc_g[half:] += o_im * u_re - o_re * u_im
            acc[...] += mm(back, pair_hat[...])

        return end

    lax.fori_loop(0, lens.shape[0], document, jnp.int32(0))
    combined, grad_product = acc[:, left], acc[:, right]
    mixer_out[...] = (query[...].astype(F32) * combined).astype(BF16)
    grad_query[...] = (cot[...].astype(F32) * combined).astype(BF16)
    grad_key[...] = (grad_product * value[...].astype(F32)).astype(BF16)
    grad_value[...] = (grad_product * key[...].astype(F32)).astype(BF16)
    g_sum = acc_g[...]
    g_hi = g_sum.astype(BF16)
    g_lo = (g_sum - g_hi.astype(F32)).astype(BF16)
    sums = mm(tap_hi[...], g_hi) + mm(tap_hi[...], g_lo) + mm(tap_lo[...], g_hi)
    tap_sums[...] = sums.astype(BF16)


def channel_block(channels):
    for block in (384, 256, 128):
        if channels % block == 0:
            return block
    return channels


def mix(doc_lengths, fields, filters, partner, owners):
    rows, channels = fields[0].shape
    taps = filters.shape[1]
    block = channel_block(channels)
    tables = fourier_tables(rows, taps, owners)
    length = 3 * rows
    field_spec = pl.BlockSpec((rows, block), lambda i: (0, i))
    filter_spec = pl.BlockSpec((block, taps), lambda i: (i, 0))
    table_specs = [pl.BlockSpec(t.shape, lambda i: (0, 0)) for t in tables]
    return pl.pallas_call(
        mix_kernel,
        grid=(channels // block,),
        in_specs=[pl.BlockSpec(memory_space=pltpu.SMEM)]
        + [field_spec] * 8
        + [filter_spec] * 2
        + table_specs,
        out_specs=[field_spec] * 4 + [pl.BlockSpec((2 * taps, block), lambda i: (0, i))],
        out_shape=[jax.ShapeDtypeStruct((rows, channels), BF16)] * 4
        + [jax.ShapeDtypeStruct((2 * taps, channels), BF16)],
        scratch_shapes=[
            pltpu.VMEM((length, block), F32),
            pltpu.VMEM((rows, 2 * block), BF16),
            pltpu.VMEM((2 * rows, 2 * block), BF16),
            pltpu.VMEM((rows, 2 * block), F32),
            pltpu.VMEM((length, block), F32),
            pltpu.VMEM((length, 2 * block), BF16),
        ],
        name="mix",
    )(doc_lengths, *fields, filters, partner, *[jnp.asarray(t) for t in tables])


def remote(src, dst, sems, index, device):
    return pltpu.make_async_remote_copy(
        src_ref=src, dst_ref=dst, send_sem=sems[0].at[index], recv_sem=sems[1].at[index],
        device_id=device, device_id_type=pl.DeviceIdType.MESH,
    )


def greet(devices):
    barrier = pltpu.get_barrier_semaphore()
    for device in devices:
        pl.semaphore_signal(barrier, inc=1, device_id=device, device_id_type=pl.DeviceIdType.MESH)
    pl.semaphore_wait(barrier, len(devices))


def spread_kernel(ctx, ch, u, r, filters, u_prev, u_next, r_prev, r_next, gathered,
                  halo_send, halo_recv, ch_send, ch_recv, core_send, core_recv, local):
    me, mine = lax.axis_index("ctx"), lax.axis_index("ch")
    after, before = {"ctx": (me + 1) % ctx}, {"ctx": (me + ctx - 1) % ctx}
    parity = me % 2
    twin = {"ctx": me + 1 - 2 * parity}
    rows = filters.shape[0] // 2
    half = pl.ds(pl.multiple_of(parity * rows, rows), rows)
    peers = [{"ch": (mine + step) % ch} for step in range(1, ch)]
    keep = pltpu.make_async_copy(filters, gathered.at[0], local)
    keep.start()
    greet([after, before] + peers)
    wide = [
        remote(filters.at[half], gathered.at[step, half], (ch_send, ch_recv), step - 1, peers[step - 1])
        for step in range(1, ch)
    ]
    for copy in wide[::-1]:
        copy.start()
    halos = [
        remote(field, place, (halo_send, halo_recv), index, device)
        for index, (field, place, device) in enumerate(
            ((u, u_prev, after), (u, u_next, before), (r, r_prev, after), (r, r_next, before))
        )
    ]
    for copy in halos:
        copy.start()
    swaps = []
    for step in range(1, ch):
        wide[step - 1].wait_recv()
        swap = remote(gathered.at[step, half], gathered.at[step, half], (core_send, core_recv), step - 1, twin)
        swap.start()
        swaps.append(swap)
    for copy in swaps:
        copy.wait()
    for copy in wide:
        copy.wait_send()
    for copy in halos:
        copy.wait()
    keep.wait()


def spread(product, upstream, filters):
    ctx, ch = lax.axis_size("ctx"), lax.axis_size("ch")
    hbm = pl.BlockSpec(memory_space=pl.ANY)
    dma = pltpu.SemaphoreType.DMA
    field = jax.ShapeDtypeStruct(product.shape, BF16)
    return pl.pallas_call(
        functools.partial(spread_kernel, ctx, ch),
        in_specs=[hbm] * 3,
        out_specs=[hbm] * 5,
        out_shape=[field] * 4 + [jax.ShapeDtypeStruct((ch, *filters.shape), BF16)],
        scratch_shapes=[dma((4,)), dma((4,)), dma((ch - 1,)), dma((ch - 1,)), dma((ch - 1,)), dma((ch - 1,)), dma],
        compiler_params=pltpu.CompilerParams(collective_id=0, has_side_effects=True),
        name="spread",
    )(product, upstream, filters)


def collect_kernel(ctx, ch, pieces, own, mirrored, landed, sent, got, sum_send, sum_recv, ch_send, ch_recv, local):
    me, mine = lax.axis_index("ctx"), lax.axis_index("ch")
    share = own.shape[0]
    others = [{"ctx": (me + step) % ctx} for step in range(1, ctx)]
    peers = [{"ch": (mine + step) % ch} for step in range(1, ch)]
    keep = pltpu.make_async_copy(pieces.at[me], landed.at[0], local)
    keep.start()
    greet(others + peers)
    copies = [
        remote(pieces.at[(me + step) % ctx], landed.at[step], (sum_send, sum_recv), step - 1, others[step - 1])
        for step in range(1, ctx)
    ]
    for copy in copies:
        copy.start()
    keep.wait()
    for copy in copies:
        copy.wait()
    sent[...] = sum(landed[step, share:].astype(F32) for step in range(ctx)).astype(BF16)
    own[...] = sum(landed[step, :share].astype(F32) for step in range(ctx))
    copies = [
        remote(sent, got.at[step - 1], (ch_send, ch_recv), step - 1, peers[step - 1]) for step in range(1, ch)
    ]
    for copy in copies:
        copy.start()
    mirrored[0] = sent[...]
    for step, copy in enumerate(copies):
        copy.wait()
        mirrored[step + 1] = got[step]


def collect(pieces):
    ctx, ch = lax.axis_size("ctx"), lax.axis_size("ch")
    _, double, channels = pieces.shape
    share = double // 2
    vmem = pl.BlockSpec(memory_space=pltpu.VMEM)
    dma = pltpu.SemaphoreType.DMA
    return pl.pallas_call(
        functools.partial(collect_kernel, ctx, ch),
        in_specs=[pl.BlockSpec(memory_space=pl.ANY)],
        out_specs=[vmem] * 2,
        out_shape=[
            jax.ShapeDtypeStruct((share, channels), F32),
            jax.ShapeDtypeStruct((ch, share, channels), BF16),
        ],
        scratch_shapes=[
            pltpu.VMEM((ctx, double, channels), BF16),
            pltpu.VMEM((share, channels), BF16),
            pltpu.VMEM((ch - 1, share, channels), BF16),
            dma((ctx - 1,)), dma((ctx - 1,)), dma((ch - 1,)), dma((ch - 1,)), dma,
        ],
        compiler_params=pltpu.CompilerParams(collective_id=1, has_side_effects=True),
        name="collect",
    )(pieces)


def shards(query_input, key_input, value_input, filters, complement, doc_lengths, cotangent):
    channels, taps = filters.shape
    ctx, ch = lax.axis_size("ctx"), lax.axis_size("ch")
    product = (key_input.astype(F32) * value_input.astype(F32)).astype(BF16)
    upstream = (cotangent.astype(F32) * query_input.astype(F32)).astype(BF16)
    *halos, gathered = spread(product, upstream, filters)

    place = (lax.axis_index("ch") - complement // channels) % ch * channels + complement % channels
    partner = jnp.take(gathered.reshape(ch * channels, taps), place, axis=0, mode="clip")
    *mixed, tap_sums = mix(
        doc_lengths, (query_input, key_input, value_input, cotangent, *halos), filters, partner, ctx
    )
    share = taps // ctx
    own, mirrored = collect(tap_sums.reshape(ctx, 2 * share, channels))
    mirrored = jnp.swapaxes(mirrored, 1, 2).reshape(ch * channels, share)
    grad_filter = own.T + jnp.take(mirrored, place, axis=0, mode="clip").astype(F32)
    return (*mixed, grad_filter)


def solution(mesh):
    placed = (
        P("ctx", "ch"),
        P("ctx", "ch"),
        P("ctx", "ch"),
        P("ch", None),
        P("ch"),
        P(),
        P("ctx", "ch"),
    )
    return jax.shard_map(
        shards,
        mesh=mesh,
        in_specs=placed,
        out_specs=(P("ctx", "ch"), P("ctx", "ch"), P("ctx", "ch"), P("ctx", "ch"), P("ch", "ctx")),
        check_vma=False,
    )
```
